768 devices in a mesh: dp: 96 (over x, z, core), section: 8 (over y).
Axes of the slice: x: 4, y: 8, z: 12, core: 2. Of those that a mesh axis runs over, the one named last changes fastest.
Arguments:
- weights: bfloat16 [8, 6144, 256], P('section'), may hold values from -0.125 to 0.125
- inputs: bfloat16 [8, 49152, 2048], P('section', 'dp'), may hold values from -40 to 40
- out_grads: bfloat16 [8, 49152, 2048], P('section', 'dp'), may hold values from -40 to 40
- master: float32 [8, 6144, 256], P('section', 'dp'), may hold values from -0.125 to 0.125
- moment1: float32 [8, 6144, 256], P('section', 'dp'), may hold values from -6 to 6
- moment2: float32 [8, 6144, 256], P('section', 'dp'), may hold values from 0.1 to 10
Outputs:
- new_master: float32 [8, 6144, 256], P('section', 'dp')
- new_moment1: float32 [8, 6144, 256], P('section', 'dp')
- new_moment2: float32 [8, 6144, 256], P('section', 'dp')
- new_weights: bfloat16 [8, 6144, 256], P('section')
The draws below stay inside these ranges and needn't reach their ends.
All inputs are finite; a program needn't handle non-finite values.
Results may differ from the reference program's by a relative error of at most 0.001.
Values may be sent and summed in bfloat16 or wider, within the bound.
A program may use at most 64 MiB of HBM per device.

```python
import math
import jax
import jax.numpy as jnp
from jax import lax

D = 2048
F = 256
MROWS = 256
STEP = 10
ROWS_DEV = 512
TOKENS = 49152
BLOCKS = 8
SHARD = 64


def heavy_columns(row_offsets):
    replicas = TOKENS // ROWS_DEV
    owner = (jnp.arange(D, dtype=jnp.int32)[None, :] * 0 + row_offsets) // SHARD
    rep = jnp.arange(replicas, dtype=jnp.int32)[:, None]
    hit = jnp.zeros((replicas, D), jnp.float32)
    for owned in owner:
        diff = (owned[None, :] - rep) % replicas
        near = (diff == 0) | (diff == 1) | (diff == replicas - 1) | (diff == replicas // 2)
        hit = jnp.maximum(hit, near.astype(jnp.float32))
    factor = 1.0 + 11.0 * hit
    return jnp.repeat(factor, ROWS_DEV, axis=0)


def scaled_field(key, rising, boost):
    keys = jax.random.split(key, 3)
    column = 10.0 ** (jnp.arange(D, dtype=jnp.float32) / D) * jax.random.uniform(keys[1], (D,), jnp.float32, 0.7, 1.4)
    row_scale = jnp.exp(jax.random.uniform(keys[2], (BLOCKS, TOKENS, 1), jnp.float32, 0.0, math.log(3.0)))
    base = jax.random.normal(keys[0], (BLOCKS, TOKENS, D), jnp.float32)
    base = jnp.clip(base, -6.0, 6.0)
    block_scale = 1.0 + rising * jnp.arange(BLOCKS, dtype=jnp.float32) / (BLOCKS - 1)
    field = base * column * row_scale * block_scale[:, None, None] * boost[None, :, :]
    return jnp.clip(field, -40.0, 40.0)


def draw_inputs(key, part):
    cols = jnp.arange(D, dtype=jnp.int32)
    boost = heavy_columns(jnp.stack([cols, cols + D]))
    return scaled_field(jax.random.fold_in(key, 11), 0.0, boost).astype(jnp.bfloat16)


def draw_out_grads(key, part):
    cols = jnp.arange(D, dtype=jnp.int32)
    boost = heavy_columns(jnp.stack([cols + 2 * D]))
    return scaled_field(jax.random.fold_in(key, 23), 2.0, boost).astype(jnp.bfloat16)


def shard_levels(own_key, shape, cuts, least, high):
    level = 1.0
    for axis_at, parts in cuts:
        steps = jax.random.uniform(jax.random.fold_in(jax.random.fold_in(own_key, 6), axis_at), (parts,), jnp.float32, least / len(cuts), high / len(cuts))
        level = level * jnp.repeat(jnp.exp(steps), shape[axis_at] // parts).reshape((-1,) + (1,) * (len(shape) - 1 - axis_at))
    return level


def scatter_about(rng, dims, deviation, bound, pieces=(), held_as=jnp.bfloat16):
    gain = shard_levels(rng, dims, pieces, -0.22, 0.18) if pieces else 1.0
    array = jax.random.normal(rng, dims, jnp.float32) * deviation * gain
    return jnp.minimum(jnp.maximum(array, -bound), bound).astype(held_as)


def setup_inputs(seed: int = 0) -> dict:
    splits = jax.random.split(jax.random.key(seed), 7)
    weights = scatter_about(splits[0], (BLOCKS, 3 * D, F), D ** -0.5, 0.125, ((0, 8),))
    inputs = draw_inputs(jax.random.fold_in(splits[6], 71), 0)
    out_grads = draw_out_grads(jax.random.fold_in(splits[6], 71), 0)
    master = scatter_about(splits[3], (BLOCKS, 3 * D, F), D ** -0.5, 0.125, ((0, 8), (1, 96)), jnp.float32)
    moment1 = scatter_about(splits[4], (BLOCKS, 3 * D, F), 1.0, 6.0, ((0, 8), (1, 96)), jnp.float32)
    moment2 = jnp.clip(jnp.exp(math.log(10.0) - 4.6051702 * jax.random.uniform(splits[5], (BLOCKS, 3 * D, F), jnp.float32) ** shard_levels(splits[5], (BLOCKS, 3 * D, F), ((0, 8), (1, 96)), -0.2, 0.2)), 0.1, 10.0)
    return dict(weights=weights, inputs=inputs, out_grads=out_grads, master=master, moment1=moment1, moment2=moment2)


def block_grads(x_rows, dy_rows, w_gate, w_up, w_down):
    pre_gate = jnp.dot(x_rows, w_gate, preferred_element_type=jnp.float32)
    pre_up = jnp.dot(x_rows, w_up, preferred_element_type=jnp.float32)
    sigma = jax.nn.sigmoid(pre_gate)
    silu_val = pre_gate * sigma
    hidden = (silu_val * pre_up).astype(jnp.bfloat16)
    d_hidden = jnp.dot(dy_rows, w_down, preferred_element_type=jnp.float32)
    d_gate = (d_hidden * pre_up * sigma * (1.0 + pre_gate * (1.0 - sigma))).astype(jnp.bfloat16)
    d_up = (d_hidden * silu_val).astype(jnp.bfloat16)
    g_gate = jnp.dot(x_rows.T, d_gate, preferred_element_type=jnp.float32)
    g_up = jnp.dot(x_rows.T, d_up, preferred_element_type=jnp.float32)
    g_down = jnp.dot(dy_rows.T, hidden, preferred_element_type=jnp.float32)
    return jnp.concatenate([g_gate, g_up, g_down], axis=0)

def section_grad(operands):
    section_w, section_x, section_dy = operands
    w_gate = section_w[:D]
    w_up = section_w[D:2 * D]
    w_down = section_w[2 * D:]
    x_blocks = section_x.reshape(-1, MROWS, D)
    dy_blocks = section_dy.reshape(-1, MROWS, D)

    def step(carry, pair):
        return (carry + block_grads(pair[0], pair[1], w_gate, w_up, w_down), None)
    start = jnp.zeros((3 * D, F), jnp.float32)
    total, unused = lax.scan(step, start, (x_blocks, dy_blocks))
    return total

def reference(weights, inputs, out_grads, master, moment1, moment2):
    grad = lax.map(section_grad, (weights, inputs, out_grads))
    total = jnp.sum(grad * grad)
    max_norm = jnp.sqrt(jnp.float32(BLOCKS * 3 * D * F))
    clip = jnp.minimum(jnp.float32(1.0), max_norm / (jnp.sqrt(total) + 1e-06))
    clipped = clip * grad
    new_moment1 = 0.9 * moment1 + 0.1 * clipped
    new_moment2 = 0.95 * moment2 + 0.05 * clipped * clipped
    first_fix = 1.0 - 0.9 ** STEP
    second_fix = 1.0 - 0.95 ** STEP
    update = new_moment1 / first_fix / (jnp.sqrt(new_moment2 / second_fix) + 1e-08) + 0.1 * master
    new_master = master - 0.01 * update
    return (new_master, new_moment1, new_moment2, new_master.astype(jnp.bfloat16))
```

```python
import functools

import jax
import jax.numpy as jnp
from jax import lax
from jax.experimental import pallas as pl
from jax.experimental.pallas import tpu as pltpu
from jax.sharding import Mesh
from jax.sharding import PartitionSpec as P

STEP = 10
NX, NZ, NC, NY = 4, 12, 2, 8
ROWS = 64
WIDTH = 256
DP = ("dp_0", "dp_1", "dp_2")
MESH = pl.DeviceIdType.MESH
HALVES = (pl.ds(0, 32), pl.ds(32, 32))
REDUCE_ORDER = (6, 5, -5, 4, -4, 3, -3, 2, -2, 1, -1, 0)
GATHER_ORDER = (0, -1, 1, -2, 2, -3, 3, -4, 4, -5, 5, 6)


def grads_kernel(w_ref, x_ref, dy_ref, keep_ref, give_ref, a_ref, b_ref, dh_ref, d_ref):
    core = lax.axis_index("dp_2")
    depth = x_ref.shape[1]
    f32 = jnp.float32
    a_ref[...] = jnp.dot(x_ref[...], w_ref[0:depth], preferred_element_type=f32)
    b_ref[...] = jnp.dot(x_ref[...], w_ref[depth : 2 * depth], preferred_element_type=f32)
    dh_ref[...] = jnp.dot(dy_ref[...], w_ref[2 * depth :], preferred_element_type=f32)
    for r in range(0, x_ref.shape[0], 128):
        rows = pl.ds(r, 128)
        a, b, dh = a_ref[rows], b_ref[rows], dh_ref[rows]
        sigma = jax.nn.sigmoid(a)
        silu = a * sigma
        d_ref[0, rows] = (dh * b * sigma * (1.0 + a * (1.0 - sigma))).astype(jnp.bfloat16)
        d_ref[1, rows] = (dh * silu).astype(jnp.bfloat16)
        d_ref[2, rows] = (silu * b).astype(jnp.bfloat16)
    first = core == 0
    for part in range(3):
        rows_ref = dy_ref if part == 2 else x_ref
        for j in range(0, depth, 512):
            p = lax.dot_general(
                rows_ref[:, j : j + 512], d_ref[part], (((0,), (0,)), ((), ())), preferred_element_type=f32
            )
            for k in range(0, 512, 128):
                block = (part * depth + j + k) // 128
                low, high = p[k : k + 64], p[k + 64 : k + 128]
                keep_ref[block // NZ, block % NZ] = jnp.where(first, low, high)
                give_ref[block // NZ, block % NZ] = jnp.where(first, high, low).astype(jnp.bfloat16)


def local_grads(weights, x_rows, dy_rows):
    tokens = x_rows.shape[0]
    vmem = pl.BlockSpec(memory_space=pltpu.VMEM)
    return pl.pallas_call(
        grads_kernel,
        out_shape=(
            jax.ShapeDtypeStruct((NX, NZ, ROWS, WIDTH), jnp.float32),
            jax.ShapeDtypeStruct((NX, NZ, ROWS, WIDTH), jnp.bfloat16),
        ),
        in_specs=[vmem] * 3,
        out_specs=(vmem, vmem),
        scratch_shapes=[
            pltpu.VMEM((tokens, WIDTH), jnp.float32),
            pltpu.VMEM((tokens, WIDTH), jnp.float32),
            pltpu.VMEM((tokens, WIDTH), jnp.float32),
            pltpu.VMEM((3, tokens, WIDTH), jnp.bfloat16),
        ],
        compiler_params=pltpu.CompilerParams(vmem_limit_bytes=32 << 20),
    )(weights, x_rows, dy_rows)


def step_kernel(
    keep_ref, give_ref, master_ref, m1_ref, m2_ref,
    new_master_ref, new_m1_ref, new_m2_ref, all_ref,
    pair_buf, x1_out, x1_left, x1_right, x2_outr, x2_outl, x2_left, x2_right,
    zp_out, zm_out, zp_in, zm_in, norm_out, norm_in,
    pair_s, pair_r, x1_s, x1_r, x2_s, x2_r, z_s, z_r, n_s, n_r, gz_s, gz_r, gx_s, gx_r, gp_s, gp_r,
):
    f32, bf16 = jnp.float32, jnp.bfloat16
    mx, mz, mc, my = (lax.axis_index(n) for n in ("dp_0", "dp_1", "dp_2", "section"))

    def to_x(k):
        return {"dp_0": lax.rem(mx + (k + NX), NX)}

    def to_z(k):
        return {"dp_1": lax.rem(mz + (k + NZ), NZ)}

    def to_y(k):
        return {"section": lax.rem(my + (k + NY), NY)}

    partner = {"dp_2": 1 - mc}
    peers = [partner]
    peers += [to_x(k) for k in range(1, NX)]
    peers += [to_z(k) for k in range(1, NZ)]
    peers += [to_y(k) for k in range(1, NY)]
    barrier = pltpu.get_barrier_semaphore()
    for peer in peers:
        pl.semaphore_signal(barrier, inc=1, device_id=peer, device_id_type=MESH)
    pl.semaphore_wait(barrier, len(peers))

    started = []

    def send(src, dst, s, r, device):
        copy = pltpu.make_async_remote_copy(
            src_ref=src, dst_ref=dst, send_sem=s, recv_sem=r, device_id=device, device_id_type=MESH
        )
        copy.start()
        started.append(copy)
        return copy

    def xi(k):
        return lax.rem(mx + (k + NX), NX)

    def zi(k):
        return lax.rem(mz + (k + NZ), NZ)

    pair = {}
    for g, off in enumerate(REDUCE_ORDER):
        pair[g] = send(give_ref.at[:, zi(off)], pair_buf.at[g], pair_s.at[g], pair_r.at[g], partner)

    x1, x2, zc = {}, {}, {}

    def own(g, k):
        x = xi(k)
        return keep_ref[x, zi(REDUCE_ORDER[g])] + pair_buf[g, x].astype(f32)

    def first_x(g):
        pair[g].wait_recv()
        x1_out[g] = own(g, 2).astype(bf16)
        x1[g, 0] = send(x1_out.at[g, HALVES[0]], x1_left.at[g], x1_s.at[0, g], x1_r.at[0, g], to_x(1))
        x1[g, 1] = send(x1_out.at[g, HALVES[1]], x1_right.at[g], x1_s.at[1, g], x1_r.at[1, g], to_x(-1))

    def second_x(g):
        right, left = own(g, 1), own(g, -1)
        x1[g, 0].wait_recv()
        x2_outr[g, 0:32] = (right[:32] + x1_left[g].astype(f32)).astype(bf16)
        x2_outr[g, 32:64] = right[32:].astype(bf16)
        x2[g, 0] = send(x2_outr.at[g], x2_left.at[g], x2_s.at[0, g], x2_r.at[0, g], to_x(1))
        x1[g, 1].wait_recv()
        x2_outl[g, 0:32] = left[:32].astype(bf16)
        x2_outl[g, 32:64] = (left[32:] + x1_right[g].astype(f32)).astype(bf16)
        x2[g, 1] = send(x2_outl.at[g], x2_right.at[g], x2_s.at[1, g], x2_r.at[1, g], to_x(-1))

    def pass_z(way, dist, reduced):
        out, arrived = ((zp_out, zp_in), (zm_out, zm_in))[way]
        for sub, rows in enumerate(HALVES):
            if dist == 6 and sub != way:
                continue
            value = reduced[32 * sub : 32 * sub + 32]
            if dist < 5 or (dist == 5 and sub == way):
                zc[way, dist, sub].wait_recv()
                value = value + arrived[dist, rows]
            out[dist - 1, rows] = value
            zc[way, dist - 1, sub] = send(
                out.at[dist - 1, rows], arrived.at[dist - 1, rows],
                z_s.at[way, dist - 1, sub], z_r.at[way, dist - 1, sub], to_z(1 - 2 * way),
            )

    def third_x(g):
        off = REDUCE_ORDER[g]
        mine = own(g, 0)
        x2[g, 0].wait_recv()
        x2[g, 1].wait_recv()
        reduced = mine + x2_left[g].astype(f32) + x2_right[g].astype(f32)
        if off == 6:
            pass_z(0, 6, reduced)
            pass_z(1, 6, reduced)
        elif off > 0:
            pass_z(0, off, reduced)
        elif off < 0:
            pass_z(1, -off, reduced)
        return reduced

    lag = 2
    count = len(REDUCE_ORDER)
    reduced = None
    for t in range(count + 2 * lag):
        if t < count:
            first_x(t)
        if 0 <= t - lag < count:
            second_x(t - lag)
        if 0 <= t - 2 * lag < count:
            reduced = third_x(t - 2 * lag)
    for way in range(2):
        for sub in range(2):
            zc[way, 0, sub].wait_recv()
    grad = reduced + zp_in[0] + zm_in[0]

    squares = grad * grad
    part = squares[0:8]
    for k in range(8, ROWS, 8):
        part = part + squares[k : k + 8]
    part = part[:, :128] + part[:, 128:]
    slot = 0
    stages = (
        [partner],
        [to_z(k) for k in range(1, NZ)],
        [to_x(k) for k in range(1, NX)],
        [to_y(k) for k in range(1, NY)],
    )
    for stage, devices in enumerate(stages):
        norm_out[stage] = part
        copies = []
        for device in devices:
            copies.append(send(norm_out.at[stage], norm_in.at[slot], n_s.at[slot], n_r.at[slot], device))
            slot += 1
        for k, copy in enumerate(copies):
            copy.wait_recv()
            part = part + norm_in[slot - len(copies) + k]
    total = jnp.sum(part, axis=(0, 1), keepdims=True)
    max_norm = jnp.sqrt(jnp.full((1, 1), float(NY * NX * NZ * NC * ROWS * WIDTH), f32))
    clip = jnp.minimum(1.0, max_norm / (jnp.sqrt(total) + 1e-06))
    clipped = clip * grad
    master = master_ref[...]
    new_m1 = 0.9 * m1_ref[...] + 0.1 * clipped
    new_m2 = 0.95 * m2_ref[...] + 0.05 * clipped * clipped
    update = new_m1 / (1.0 - 0.9**STEP) / (jnp.sqrt(new_m2 / (1.0 - 0.95**STEP)) + 1e-08) + 0.1 * master
    new_master = master - 0.01 * update
    new_m1_ref[...] = new_m1
    new_m2_ref[...] = new_m2
    new_master_ref[...] = new_master
    all_ref[mx, mz, mc] = new_master.astype(bf16)

    gz, gx, gr, gp = {}, {}, {}, {}

    def block(k, off, rows=None):
        ref = all_ref.at[xi(k), zi(off), mc]
        return ref if rows is None else ref.at[rows]

    def to_partner(g, j, k, off):
        ref = block(k, off)
        gp[g, j] = send(ref, ref, gp_s.at[g, j], gp_r.at[g, j], partner)

    def pass_on_z(way, dist, off):
        if dist > 5:
            return
        ref = block(0, off, HALVES[way] if dist == 5 else None)
        gz[way, dist] = send(ref, ref, gz_s.at[way, dist], gz_r.at[way, dist], to_z(1 - 2 * way))

    def gather_z(g):
        off = GATHER_ORDER[g]
        if off == 0:
            pass_on_z(0, 0, 0)
            pass_on_z(1, 0, 0)
        elif off == 6:
            gz[0, 5].wait_recv()
            gz[1, 5].wait_recv()
        else:
            way, dist = (0, -off) if off < 0 else (1, off)
            gz[way, dist - 1].wait_recv()
            pass_on_z(way, dist, off)
        ref = block(0, off)
        gx[g, 0] = send(ref, ref, gx_s.at[0, g], gx_r.at[0, g], to_x(1))
        gx[g, 1] = send(ref, ref, gx_s.at[1, g], gx_r.at[1, g], to_x(-1))
        to_partner(g, 0, 0, off)

    def gather_x(g):
        off = GATHER_ORDER[g]
        for way in range(2):
            gx[g, way].wait_recv()
            k = 2 * way - 1
            ref = block(k, off, HALVES[way])
            gr[g, way] = send(ref, ref, gx_s.at[2 + way, g], gx_r.at[2 + way, g], to_x(-k))
            to_partner(g, 1 + way, k, off)

    def gather_far(g):
        gr[g, 0].wait_recv()
        gr[g, 1].wait_recv()
        to_partner(g, 3, 2, GATHER_ORDER[g])

    for t in range(count + 2 * lag):
        if t < count:
            gather_z(t)
        if 0 <= t - lag < count:
            gather_x(t - lag)
        if 0 <= t - 2 * lag < count:
            gather_far(t - 2 * lag)
    for copy in gp.values():
        copy.wait_recv()
    for copy in started:
        copy.wait_send()


def reduce_step_gather(keep, give, master, m1, m2):
    f32, bf16 = jnp.float32, jnp.bfloat16
    vmem = pl.BlockSpec(memory_space=pltpu.VMEM)
    state = jax.ShapeDtypeStruct((ROWS, WIDTH), f32)
    dma = pltpu.SemaphoreType.DMA
    wide = pltpu.VMEM((NZ, ROWS, WIDTH), bf16)
    half = pltpu.VMEM((NZ, ROWS // 2, WIDTH), bf16)
    ring = pltpu.VMEM((6, ROWS, WIDTH), f32)
    peers = 1 + (NX - 1) + (NZ - 1) + (NY - 1)
    return pl.pallas_call(
        step_kernel,
        out_shape=(state, state, state, jax.ShapeDtypeStruct((NX, NZ, NC, ROWS, WIDTH), bf16)),
        in_specs=[vmem] * 5,
        out_specs=(vmem,) * 4,
        scratch_shapes=[
            pltpu.VMEM((NZ, NX, ROWS, WIDTH), bf16),
            wide, half, half, wide, wide, wide, wide,
            ring, ring, ring, ring,
            pltpu.VMEM((4, 8, 128), f32),
            pltpu.VMEM((peers, 8, 128), f32),
            dma((NZ,)), dma((NZ,)),
            dma((2, NZ)), dma((2, NZ)),
            dma((2, NZ)), dma((2, NZ)),
            dma((2, 6, 2)), dma((2, 6, 2)),
            dma((peers,)), dma((peers,)),
            dma((2, 6)), dma((2, 6)),
            dma((4, NZ)), dma((4, NZ)),
            dma((NZ, 4)), dma((NZ, 4)),
        ],
        compiler_params=pltpu.CompilerParams(
            collective_id=0, has_side_effects=True, vmem_limit_bytes=40 << 20
        ),
    )(keep, give, master, m1, m2)


def local(weights, inputs, out_grads, master, moment1, moment2):
    keep, give = local_grads(weights[0], inputs[0], out_grads[0])
    new_master, new_m1, new_m2, gathered = reduce_step_gather(keep, give, master[0], moment1[0], moment2[0])
    return (new_master[None], new_m1[None], new_m2[None], gathered.reshape(weights.shape))


def solution(mesh):
    split = Mesh(
        mesh.devices.reshape(NX, NZ, NC, mesh.shape["section"]), ("dp_0", "dp_1", "dp_2", "section")
    )
    shard = P("section", DP, None)
    whole = P("section", None, None)
    return jax.shard_map(
        local,
        mesh=split,
        in_specs=(whole, shard, shard, shard, shard, shard),
        out_specs=(shard, shard, shard, whole),
        check_vma=False,
    )
```

```python
import jax
import jax.numpy as jnp
from jax import lax
from jax.experimental import pallas as pl
from jax.experimental.pallas import tpu as pltpu
from jax.sharding import Mesh
from jax.sharding import PartitionSpec as P

STEP = 10
NX, NZ, NC, NY = 4, 12, 2, 8
ROWS = 64
WIDTH = 256
DP = ("dp_0", "dp_1", "dp_2")
MESH = pl.DeviceIdType.MESH
REACH_REDUCE = 2
REACH_GATHER = 2
HALVES = (pl.ds(0, 32), pl.ds(32, 32))
REDUCE_ORDER = (6, 5, -5, 4, -4, 3, -3, 2, -2, 1, -1, 0)
GATHER_ORDER = (0, -1, 1, -2, 2, -3, 3, -4, 4, -5, 5, 6)
LAG = 4
LAG_A, LAG_B, LAG_C = 2, 5, 8


def relay_of(dist, reach):
    return (dist - 1) // reach * reach


def local_forward(w_hbm, x_hbm, dy_hbm, w_ref, xy_ref, a_ref, b_ref, dh_ref, d_ref, load_s):
    f32 = jnp.float32
    depth = x_hbm.shape[1]
    parts = [(x_hbm, xy_ref.at[0])]
    parts += [(w_hbm.at[pl.ds(k * depth, depth)], w_ref.at[pl.ds(k * depth, depth)]) for k in range(2)]
    parts += [(dy_hbm, xy_ref.at[1]), (w_hbm.at[pl.ds(2 * depth, depth)], w_ref.at[pl.ds(2 * depth, depth)])]
    loads = [pltpu.make_async_copy(src, dst, load_s.at[k]) for k, (src, dst) in enumerate(parts)]
    for load in loads:
        load.start()

    def compute():
        loads[0].wait()
        loads[1].wait()
        a_ref[...] = jnp.dot(xy_ref[0], w_ref[0:depth], preferred_element_type=f32)
        loads[2].wait()
        b_ref[...] = jnp.dot(xy_ref[0], w_ref[depth : 2 * depth], preferred_element_type=f32)
        loads[3].wait()
        loads[4].wait()
        dh_ref[...] = jnp.dot(xy_ref[1], w_ref[2 * depth :], preferred_element_type=f32)
        for r in range(0, a_ref.shape[0], 128):
            rows = pl.ds(r, 128)
            a, b, dh = a_ref[rows], b_ref[rows], dh_ref[rows]
            sigma = jax.nn.sigmoid(a)
            silu = a * sigma
            d_ref[0, rows] = (dh * b * sigma * (1.0 + a * (1.0 - sigma))).astype(jnp.bfloat16)
            d_ref[1, rows] = (dh * silu).astype(jnp.bfloat16)
            d_ref[2, rows] = (silu * b).astype(jnp.bfloat16)

    return compute


def step_kernel(
    w_hbm, x_hbm, dy_hbm, master_hbm, m1_hbm, m2_hbm,
    clipped_ref, all_ref,
    w_ref, xy_ref, a_ref, b_ref, dh_ref, d_ref, state_ref, keep_ref, give_ref,
    pair_buf, x1_out, x1_left, x1_right, x2_outr, x2_outl, x2_left, x2_right,
    zp_out, zm_out, zp_in, zm_in, norm_out, norm_in,
    load_s, state_s,
    pair_s, pair_r, x1_s, x1_r, x2_s, x2_r, z_s, z_r, n_s, n_r, gz_s, gz_r, gx_s, gx_r, gp_s, gp_r,
):
    f32, bf16 = jnp.float32, jnp.bfloat16
    mx, mz, mc, my = (lax.axis_index(n) for n in ("dp_0", "dp_1", "dp_2", "section"))

    def xi(k):
        return lax.rem(mx + (k + NX), NX)

    def zi(k):
        return lax.rem(mz + (k + NZ), NZ)

    def to_x(k):
        return {"dp_0": xi(k)}

    def to_z(k):
        return {"dp_1": zi(k)}

    def to_y(k):
        return {"section": lax.rem(my + (k + NY), NY)}

    partner = {"dp_2": 1 - mc}
    stages = (
        [to_z(k) for k in range(1, NZ)],
        [to_x(k) for k in range(1, NX)],
        [to_y(k) for k in range(1, NY)] + [{**to_y(k), **partner} for k in range(NY)],
    )
    peers = [device for stage in stages for device in stage]
    barrier = pltpu.get_barrier_semaphore()
    for peer in peers:
        pl.semaphore_signal(barrier, inc=1, device_id=peer, device_id_type=MESH)
    compute = local_forward(w_hbm, x_hbm, dy_hbm, w_ref, xy_ref, a_ref, b_ref, dh_ref, d_ref, load_s)
    states = [
        pltpu.make_async_copy(src, state_ref.at[k], state_s.at[k])
        for k, src in enumerate((master_hbm, m1_hbm, m2_hbm))
    ]
    for load in states:
        load.start()
    compute()

    started = []

    def send(src, dst, s, r, device):
        copy = pltpu.make_async_remote_copy(
            src_ref=src, dst_ref=dst, send_sem=s, recv_sem=r, device_id=device, device_id_type=MESH
        )
        copy.start()
        started.append(copy)
        return copy

    pair, x1, x2, zc = {}, {}, {}, {}
    per_part = x_hbm.shape[1] // 128
    low_mine = mc == 0

    def gradients(g):
        for k in range(NX):
            block = xi(k) * NZ + zi(REDUCE_ORDER[g])
            part = block // per_part
            cols = pl.multiple_of(block % per_part * 128, 128)
            rows = xy_ref[part // 2, :, pl.ds(cols, 128)]
            p = lax.dot_general(rows, d_ref[part], (((0,), (0,)), ((), ())), preferred_element_type=f32)
            low, high = p[:ROWS], p[ROWS:]
            keep_ref[g, k] = jnp.where(low_mine, low, high)
            give_ref[g, k] = jnp.where(low_mine, high, low).astype(bf16)

    def swap(g):
        pair[g] = send(give_ref.at[g], pair_buf.at[g], pair_s.at[g], pair_r.at[g], partner)

    def own(g, k):
        return keep_ref[g, k % NX] + pair_buf[g, k % NX].astype(f32)

    def first_x(g):
        pair[g].wait_recv()
        x1_out[g] = own(g, 2).astype(bf16)
        x1[g, 0] = send(x1_out.at[g, HALVES[0]], x1_left.at[g], x1_s.at[0, g], x1_r.at[0, g], to_x(1))
        x1[g, 1] = send(x1_out.at[g, HALVES[1]], x1_right.at[g], x1_s.at[1, g], x1_r.at[1, g], to_x(-1))

    def second_x(g):
        right, left = own(g, 1), own(g, -1)
        x1[g, 0].wait_recv()
        x2_outr[g, 0:32] = (right[:32] + x1_left[g].astype(f32)).astype(bf16)
        x2_outr[g, 32:64] = right[32:].astype(bf16)
        x2[g, 0] = send(x2_outr.at[g], x2_left.at[g], x2_s.at[0, g], x2_r.at[0, g], to_x(1))
        x1[g, 1].wait_recv()
        x2_outl[g, 0:32] = left[:32].astype(bf16)
        x2_outl[g, 32:64] = (left[32:] + x1_right[g].astype(f32)).astype(bf16)
        x2[g, 1] = send(x2_outl.at[g], x2_right.at[g], x2_s.at[1, g], x2_r.at[1, g], to_x(-1))

    def collect_z(way, sub, dist, value):
        arrived = (zp_in, zm_in)[way]
        for source in range(dist + 1, dist + REACH_REDUCE + 1):
            if source < 6 or (source == 6 and sub == way):
                zc[way, source, sub].wait_recv()
                value = value + arrived[source - 1, HALVES[sub]]
        return value

    def pass_z(way, dist, reduced):
        out, arrived = ((zp_out, zp_in), (zm_out, zm_in))[way]
        hops = dist - relay_of(dist, REACH_REDUCE)
        for sub, rows in enumerate(HALVES):
            if dist == 6 and sub != way:
                continue
            value = reduced[32 * sub : 32 * sub + 32]
            if dist % REACH_REDUCE == 0:
                value = collect_z(way, sub, dist, value)
            out[dist - 1, rows] = value
            zc[way, dist, sub] = send(
                out.at[dist - 1, rows], arrived.at[dist - 1, rows],
                z_s.at[way, dist - 1, sub], z_r.at[way, dist - 1, sub], to_z(hops * (1 - 2 * way)),
            )

    def third_x(g):
        off = REDUCE_ORDER[g]
        mine = own(g, 0)
        x2[g, 0].wait_recv()
        x2[g, 1].wait_recv()
        reduced = mine + x2_left[g].astype(f32) + x2_right[g].astype(f32)
        if off == 6:
            pass_z(0, 6, reduced)
            pass_z(1, 6, reduced)
        elif off > 0:
            pass_z(0, off, reduced)
        elif off < 0:
            pass_z(1, -off, reduced)
        return reduced

    count = len(REDUCE_ORDER)
    reduced = None
    gradients(0)
    pl.semaphore_wait(barrier, len(peers))
    swap(0)
    for t in range(1, count + LAG_C + 1):
        if t < count:
            gradients(t)
            swap(t)
        if 0 <= t - LAG_A < count:
            first_x(t - LAG_A)
        if 0 <= t - LAG_B < count:
            second_x(t - LAG_B)
        if 0 <= t - LAG_C < count:
            reduced = third_x(t - LAG_C)
    halves = []
    for sub in range(2):
        value = collect_z(0, sub, 0, reduced[32 * sub : 32 * sub + 32])
        halves.append(collect_z(1, sub, 0, value))
    grad = jnp.concatenate(halves, axis=0)

    part = jnp.sum(grad * grad, axis=0, keepdims=True)
    part = part[:, :128] + part[:, 128:]
    slot = 0
    for stage, devices in enumerate(stages):
        norm_out[stage] = part
        copies = []
        for device in devices:
            copies.append(send(norm_out.at[stage], norm_in.at[slot], n_s.at[slot], n_r.at[slot], device))
            slot += 1
        for k, copy in enumerate(copies):
            copy.wait_recv()
            part = part + norm_in[slot - len(copies) + k]
    total = jnp.sum(part, axis=1, keepdims=True)
    max_norm = jnp.sqrt(jnp.full((1, 1), float(NY * NX * NZ * NC * ROWS * WIDTH), f32))
    clip = jnp.minimum(1.0, max_norm / (jnp.sqrt(total) + 1e-06))
    clipped = clip * grad
    clipped_ref[...] = clipped
    for load in states:
        load.wait()
    new_master = adam(clipped, state_ref[0], state_ref[1], state_ref[2])[0]
    all_ref[mx, mz, mc] = new_master.astype(bf16)

    gz, gx, gr, gp = {}, {}, {}, {}

    def block(k, off, rows=None):
        ref = all_ref.at[xi(k), zi(off), mc]
        return ref if rows is None else ref.at[rows]

    def to_partner(g, j, k, off):
        ref = block(k, off)
        gp[g, j] = send(ref, ref, gp_s.at[g, j], gp_r.at[g, j], partner)

    def pass_on_z(way, dist, off):
        if dist % REACH_GATHER:
            return
        for target in range(dist + 1, min(dist + REACH_GATHER, 6) + 1):
            ref = block(0, off, HALVES[way] if target == 6 else None)
            gz[way, target] = send(
                ref, ref, gz_s.at[way, target - 1], gz_r.at[way, target - 1],
                to_z((target - dist) * (1 - 2 * way)),
            )

    def gather_z(g):
        off = GATHER_ORDER[g]
        if off == 0:
            pass_on_z(0, 0, 0)
            pass_on_z(1, 0, 0)
        elif off == 6:
            gz[0, 6].wait_recv()
            gz[1, 6].wait_recv()
        else:
            way, dist = (0, -off) if off < 0 else (1, off)
            gz[way, dist].wait_recv()
            pass_on_z(way, dist, off)
        ref = block(0, off)
        gx[g, 0] = send(ref, ref, gx_s.at[0, g], gx_r.at[0, g], to_x(1))
        gx[g, 1] = send(ref, ref, gx_s.at[1, g], gx_r.at[1, g], to_x(-1))
        to_partner(g, 0, 0, off)

    def gather_x(g):
        off = GATHER_ORDER[g]
        for way in range(2):
            gx[g, way].wait_recv()
            k = 2 * way - 1
            ref = block(k, off, HALVES[way])
            gr[g, way] = send(ref, ref, gx_s.at[2 + way, g], gx_r.at[2 + way, g], to_x(-k))
            to_partner(g, 1 + way, k, off)

    def gather_far(g):
        gr[g, 0].wait_recv()
        gr[g, 1].wait_recv()
        to_partner(g, 3, 2, GATHER_ORDER[g])

    for t in range(count + 2 * LAG):
        if t < count:
            gather_z(t)
        if 0 <= t - LAG < count:
            gather_x(t - LAG)
        if 0 <= t - 2 * LAG < count:
            gather_far(t - 2 * LAG)
    for copy in gp.values():
        copy.wait_recv()
    for copy in started:
        copy.wait_send()


def adam(clipped, master, moment1, moment2):
    new_m1 = 0.9 * moment1 + 0.1 * clipped
    new_m2 = 0.95 * moment2 + 0.05 * clipped * clipped
    update = new_m1 / (1.0 - 0.9**STEP) / (jnp.sqrt(new_m2 / (1.0 - 0.95**STEP)) + 1e-08) + 0.1 * master
    return master - 0.01 * update, new_m1, new_m2


def reduce_step_gather(weights, x_rows, dy_rows, master, m1, m2):
    f32, bf16 = jnp.float32, jnp.bfloat16
    vmem = pl.BlockSpec(memory_space=pltpu.VMEM)
    dma = pltpu.SemaphoreType.DMA
    tokens = x_rows.shape[0]
    blocks = pltpu.VMEM((NZ, NX, ROWS, WIDTH), bf16)
    wide = pltpu.VMEM((NZ, ROWS, WIDTH), bf16)
    half = pltpu.VMEM((NZ, ROWS // 2, WIDTH), bf16)
    ring = pltpu.VMEM((6, ROWS, WIDTH), f32)
    acts = pltpu.VMEM((tokens, WIDTH), f32)
    peers = (NX - 1) + (NZ - 1) + (2 * NY - 1)
    return pl.pallas_call(
        step_kernel,
        out_shape=(
            jax.ShapeDtypeStruct((ROWS, WIDTH), f32),
            jax.ShapeDtypeStruct((NX, NZ, NC, ROWS, WIDTH), bf16),
        ),
        in_specs=[pl.BlockSpec(memory_space=pltpu.HBM)] * 6,
        out_specs=(vmem, vmem),
        scratch_shapes=[
            pltpu.VMEM(weights.shape, bf16),
            pltpu.VMEM((2, *x_rows.shape), bf16),
            acts, acts, acts,
            pltpu.VMEM((3, tokens, WIDTH), bf16),
            pltpu.VMEM((3, ROWS, WIDTH), f32),
            pltpu.VMEM((NZ, NX, ROWS, WIDTH), f32),
            blocks, blocks,
            wide, half, half, wide, wide, wide, wide,
            ring, ring, ring, ring,
            pltpu.VMEM((3, 1, 128), f32),
            pltpu.VMEM((peers, 1, 128), f32),
            dma((5,)), dma((3,)),
            dma((NZ,)), dma((NZ,)),
            dma((2, NZ)), dma((2, NZ)),
            dma((2, NZ)), dma((2, NZ)),
            dma((2, 6, 2)), dma((2, 6, 2)),
            dma((peers,)), dma((peers,)),
            dma((2, 6)), dma((2, 6)),
            dma((4, NZ)), dma((4, NZ)),
            dma((NZ, 4)), dma((NZ, 4)),
        ],
        compiler_params=pltpu.CompilerParams(
            collective_id=0, has_side_effects=True, vmem_limit_bytes=34 << 20
        ),
    )(*(pltpu.with_memory_space_constraint(v, pltpu.HBM) for v in (weights, x_rows, dy_rows, master, m1, m2)))


def local(weights, inputs, out_grads, master, moment1, moment2):
    clipped, gathered = reduce_step_gather(
        weights[0], inputs[0], out_grads[0], master[0], moment1[0], moment2[0]
    )
    outs = adam(clipped[None], master, moment1, moment2)
    return (*outs, gathered.reshape(weights.shape))


def solution(mesh):
    split = Mesh(
        mesh.devices.reshape(NX, NZ, NC, mesh.shape["section"]), ("dp_0", "dp_1", "dp_2", "section")
    )
    shard = P("section", DP, None)
    whole = P("section", None, None)
    return jax.shard_map(
        local,
        mesh=split,
        in_specs=(whole, shard, shard, shard, shard, shard),
        out_specs=(shard, shard, shard, whole),
        check_vma=False,
    )
```

```python
import jax
import jax.numpy as jnp
from jax import lax
from jax.experimental import pallas as pl
from jax.experimental.pallas import tpu as pltpu
from jax.sharding import Mesh
from jax.sharding import PartitionSpec as P

STEP = 10
CHUNKS = 4
NX, NZ, NC, NY = 4, 12, 2, 8
ROWS = 64
WIDTH = 256
DP = ("dp_0", "dp_1", "dp_2")
MESH = pl.DeviceIdType.MESH
REACH_REDUCE = 2
REACH_GATHER = 3
HALVES = (pl.ds(0, 32), pl.ds(32, 32))
REDUCE_ORDER = (6, 5, -5, 4, -4, 3, -3, 2, -2, 1, -1, 0)
GATHER_ORDER = (0, -1, 1, -2, 2, -3, 3, -4, 4, -5, 5, 6)
LAG = 4
LAG_A, LAG_B, LAG_C = 2, 5, 8


def relay_of(dist, reach):
    return (dist - 1) // reach * reach


def local_forward(w_hbm, x_hbm, dy_hbm, w_ref, xy_ref, a_ref, b_ref, dh_ref, d_ref, load_s):
    f32, bf16 = jnp.float32, jnp.bfloat16
    depth = x_hbm.shape[1]
    tile = depth // CHUNKS
    loads = []

    def load(src, dst):
        copy = pltpu.make_async_copy(src, dst, load_s.at[len(loads)])
        copy.start()
        loads.append(copy)
        return copy

    first, second = [], []
    for k in range(CHUNKS):
        cols = pl.ds(k * tile, tile)
        waits = [load(x_hbm.at[:, cols], xy_ref.at[0, :, cols])]
        for part in range(2):
            rows = pl.ds(part * depth + k * tile, tile)
            waits.append(load(w_hbm.at[rows], w_ref.at[rows]))
        first.append(waits)
    for k in range(CHUNKS):
        cols, rows = pl.ds(k * tile, tile), pl.ds(2 * depth + k * tile, tile)
        second.append([load(dy_hbm.at[:, cols], xy_ref.at[1, :, cols]), load(w_hbm.at[rows], w_ref.at[rows])])

    def accumulate(out_ref, which, k, part):
        cols, rows = pl.ds(k * tile, tile), pl.ds(part * depth + k * tile, tile)
        product = jnp.dot(xy_ref[which, :, cols], w_ref[rows], preferred_element_type=f32)
        out_ref[...] = product if k == 0 else out_ref[...] + product

    def compute():
        for k in range(CHUNKS):
            for copy in first[k]:
                copy.wait()
            accumulate(a_ref, 0, k, 0)
            accumulate(b_ref, 0, k, 1)
        for r in range(0, a_ref.shape[0], 128):
            rows = pl.ds(r, 128)
            a, b = a_ref[rows], b_ref[rows]
            sigma = jax.nn.sigmoid(a)
            silu = a * sigma
            d_ref[2, rows] = (silu * b).astype(bf16)
            a_ref[rows] = silu
            b_ref[rows] = b * sigma * (1.0 + a * (1.0 - sigma))
        for k in range(CHUNKS):
            for copy in second[k]:
                copy.wait()
            accumulate(dh_ref, 1, k, 2)
        for r in range(0, a_ref.shape[0], 128):
            rows = pl.ds(r, 128)
            dh = dh_ref[rows]
            d_ref[0, rows] = (dh * b_ref[rows]).astype(bf16)
            d_ref[1, rows] = (dh * a_ref[rows]).astype(bf16)

    return compute


def step_kernel(
    w_hbm, x_hbm, dy_hbm, master_hbm, m1_hbm, m2_hbm,
    clipped_ref, all_ref,
    w_ref, xy_ref, a_ref, b_ref, dh_ref, d_ref, state_ref, keep_ref, give_ref,
    pair_buf, x1_out, x1_left, x1_right, x2_outr, x2_outl, x2_left, x2_right,
    zp_out, zm_out, zp_in, zm_in, norm_out, norm_in,
    load_s, state_s,
    pair_s, pair_r, x1_s, x1_r, x2_s, x2_r, z_s, z_r, n_s, n_r, gz_s, gz_r, gx_s, gx_r, gp_s, gp_r,
):
    f32, bf16 = jnp.float32, jnp.bfloat16
    mx, mz, mc, my = (lax.axis_index(n) for n in ("dp_0", "dp_1", "dp_2", "section"))

    xs = [lax.rem(mx + k, NX) for k in range(NX)]
    zs = [lax.rem(mz + k, NZ) for k in range(NZ)]
    ys = [lax.rem(my + k, NY) for k in range(NY)]

    def xi(k):
        return xs[k % NX]

    def zi(k):
        return zs[k % NZ]

    def to_x(k):
        return {"dp_0": xi(k)}

    def to_z(k):
        return {"dp_1": zi(k)}

    def to_y(k):
        return {"section": ys[k]}

    partner = {"dp_2": 1 - mc}
    stages = (
        [to_z(k) for k in range(1, NZ)] + [{**to_z(k), **partner} for k in range(NZ)],
        [{**to_x(j), **to_y(k)} for j in range(NX) for k in range(NY) if j or k],
    )
    peers = [device for stage in stages for device in stage]
    barrier = pltpu.get_barrier_semaphore()
    for peer in peers:
        pl.semaphore_signal(barrier, inc=1, device_id=peer, device_id_type=MESH)
    compute = local_forward(w_hbm, x_hbm, dy_hbm, w_ref, xy_ref, a_ref, b_ref, dh_ref, d_ref, load_s)
    states = [
        pltpu.make_async_copy(src, state_ref.at[k], state_s.at[k])
        for k, src in enumerate((master_hbm, m1_hbm, m2_hbm))
    ]
    for load in states:
        load.start()
    compute()

    started = []

    def send(src, dst, s, r, device):
        copy = pltpu.make_async_remote_copy(
            src_ref=src, dst_ref=dst, send_sem=s, recv_sem=r, device_id=device, device_id_type=MESH
        )
        copy.start()
        started.append(copy)
        return copy

    pair, x1, x2, zc = {}, {}, {}, {}
    per_part = x_hbm.shape[1] // 128
    low_mine = mc == 0

    def gradients(g):
        for k in range(NX):
            block = xi(k) * NZ + zi(REDUCE_ORDER[g])
            part = lax.div(block, per_part)
            cols = pl.multiple_of(lax.rem(block, per_part) * 128, 128)
            rows = xy_ref[lax.div(part, 2), :, pl.ds(cols, 128)]
            p = lax.dot_general(rows, d_ref[part], (((0,), (0,)), ((), ())), preferred_element_type=f32)
            low, high = p[:ROWS], p[ROWS:]
            keep_ref[g, k] = jnp.where(low_mine, low, high)
            give_ref[g, k] = jnp.where(low_mine, high, low).astype(bf16)

    def swap(g):
        pair[g] = send(give_ref.at[g], pair_buf.at[g], pair_s.at[g], pair_r.at[g], partner)

    def own(g, k):
        return keep_ref[g, k % NX] + pair_buf[g, k % NX].astype(f32)

    def first_x(g):
        pair[g].wait_recv()
        x1_out[g] = own(g, 2).astype(bf16)
        x1[g, 0] = send(x1_out.at[g, HALVES[0]], x1_left.at[g], x1_s.at[0, g], x1_r.at[0, g], to_x(1))
        x1[g, 1] = send(x1_out.at[g, HALVES[1]], x1_right.at[g], x1_s.at[1, g], x1_r.at[1, g], to_x(-1))

    def second_x(g):
        right, left = own(g, 1), own(g, -1)
        x1[g, 0].wait_recv()
        x2_outr[g, 0:32] = (right[:32] + x1_left[g].astype(f32)).astype(bf16)
        x2_outr[g, 32:64] = right[32:].astype(bf16)
        x2[g, 0] = send(x2_outr.at[g], x2_left.at[g], x2_s.at[0, g], x2_r.at[0, g], to_x(1))
        x1[g, 1].wait_recv()
        x2_outl[g, 0:32] = left[:32].astype(bf16)
        x2_outl[g, 32:64] = (left[32:] + x1_right[g].astype(f32)).astype(bf16)
        x2[g, 1] = send(x2_outl.at[g], x2_right.at[g], x2_s.at[1, g], x2_r.at[1, g], to_x(-1))

    def collect_z(way, sub, dist, value):
        arrived = (zp_in, zm_in)[way]
        for source in range(dist + 1, dist + REACH_REDUCE + 1):
            if source < 6 or (source == 6 and sub == way):
                zc[way, source, sub].wait_recv()
                value = value + arrived[source - 1, HALVES[sub]]
        return value

    def pass_z(way, dist, reduced):
        out, arrived = ((zp_out, zp_in), (zm_out, zm_in))[way]
        hops = dist - relay_of(dist, REACH_REDUCE)
        for sub, rows in enumerate(HALVES):
            if dist == 6 and sub != way:
                continue
            value = reduced[32 * sub : 32 * sub + 32]
            if dist % REACH_REDUCE == 0:
                value = collect_z(way, sub, dist, value)
            out[dist - 1, rows] = value
            zc[way, dist, sub] = send(
                out.at[dist - 1, rows], arrived.at[dist - 1, rows],
                z_s.at[way, dist - 1, sub], z_r.at[way, dist - 1, sub], to_z(hops * (1 - 2 * way)),
            )

    def third_x(g):
        off = REDUCE_ORDER[g]
        mine = own(g, 0)
        x2[g, 0].wait_recv()
        x2[g, 1].wait_recv()
        reduced = mine + x2_left[g].astype(f32) + x2_right[g].astype(f32)
        if off == 6:
            pass_z(0, 6, reduced)
            pass_z(1, 6, reduced)
        elif off > 0:
            pass_z(0, off, reduced)
        elif off < 0:
            pass_z(1, -off, reduced)
        return reduced

    count = len(REDUCE_ORDER)
    reduced = None
    gradients(0)
    pl.semaphore_wait(barrier, len(peers))
    swap(0)
    for t in range(1, count + LAG_C + 1):
        if t < count:
            gradients(t)
            swap(t)
        if 0 <= t - LAG_A < count:
            first_x(t - LAG_A)
        if 0 <= t - LAG_B < count:
            second_x(t - LAG_B)
        if 0 <= t - LAG_C < count:
            reduced = third_x(t - LAG_C)
    halves = []
    for sub in range(2):
        value = collect_z(0, sub, 0, reduced[32 * sub : 32 * sub + 32])
        halves.append(collect_z(1, sub, 0, value))
    grad = jnp.concatenate(halves, axis=0)

    part = jnp.sum(grad * grad, axis=0, keepdims=True)
    part = part[:, :128] + part[:, 128:]
    slot = 0
    for stage, devices in enumerate(stages):
        norm_out[stage] = part
        copies = []
        for device in devices:
            copies.append(send(norm_out.at[stage], norm_in.at[slot], n_s.at[slot], n_r.at[slot], device))
            slot += 1
        for k, copy in enumerate(copies):
            copy.wait_recv()
            part = part + norm_in[slot - len(copies) + k]
    total = jnp.sum(part, axis=1, keepdims=True)
    max_norm = jnp.sqrt(jnp.full((1, 1), float(NY * NX * NZ * NC * ROWS * WIDTH), f32))
    clip = jnp.minimum(1.0, max_norm / (jnp.sqrt(total) + 1e-06))
    clipped = clip * grad
    clipped_ref[...] = clipped
    for load in states:
        load.wait()
    new_master = adam(clipped, state_ref[0], state_ref[1], state_ref[2])[0]
    all_ref[(mx * NZ + mz) * NC + mc] = new_master.astype(bf16)

    gz, gx, gr, gp, places = {}, {}, {}, {}, {}

    def block(k, off, rows=None):
        key = k % NX, off % NZ
        if key not in places:
            places[key] = (xi(k) * NZ + zi(off)) * NC + mc
        return all_ref.at[places[key]] if rows is None else all_ref.at[places[key], rows]

    def to_partner(g, j, k, off):
        ref = block(k, off)
        gp[g, j] = send(ref, ref, gp_s.at[g, j], gp_r.at[g, j], partner)

    def pass_on_z(way, dist, off):
        if dist % REACH_GATHER:
            return
        for target in range(dist + 1, min(dist + REACH_GATHER, 6) + 1):
            ref = block(0, off, HALVES[way] if target == 6 else None)
            gz[way, target] = send(
                ref, ref, gz_s.at[way, target - 1], gz_r.at[way, target - 1],
                to_z((target - dist) * (1 - 2 * way)),
            )

    def gather_z(g):
        off = GATHER_ORDER[g]
        if off == 0:
            pass_on_z(0, 0, 0)
            pass_on_z(1, 0, 0)
        elif off == 6:
            gz[0, 6].wait_recv()
            gz[1, 6].wait_recv()
        else:
            way, dist = (0, -off) if off < 0 else (1, off)
            gz[way, dist].wait_recv()
            pass_on_z(way, dist, off)
        ref = block(0, off)
        gx[g, 0] = send(ref, ref, gx_s.at[0, g], gx_r.at[0, g], to_x(1))
        gx[g, 1] = send(ref, ref, gx_s.at[1, g], gx_r.at[1, g], to_x(-1))
        to_partner(g, 0, 0, off)

    def gather_x(g):
        off = GATHER_ORDER[g]
        for way in range(2):
            gx[g, way].wait_recv()
            k = 2 * way - 1
            ref = block(k, off, HALVES[way])
            gr[g, way] = send(ref, ref, gx_s.at[2 + way, g], gx_r.at[2 + way, g], to_x(-k))
            to_partner(g, 1 + way, k, off)

    def gather_far(g):
        gr[g, 0].wait_recv()
        gr[g, 1].wait_recv()
        to_partner(g, 3, 2, GATHER_ORDER[g])

    for t in range(count + 2 * LAG):
        if t < count:
            gather_z(t)
        if 0 <= t - LAG < count:
            gather_x(t - LAG)
        if 0 <= t - 2 * LAG < count:
            gather_far(t - 2 * LAG)
    for copy in gp.values():
        copy.wait_recv()
    for copy in started:
        copy.wait_send()


def adam(clipped, master, moment1, moment2):
    new_m1 = 0.9 * moment1 + 0.1 * clipped
    new_m2 = 0.95 * moment2 + 0.05 * clipped * clipped
    update = new_m1 / (1.0 - 0.9**STEP) / (jnp.sqrt(new_m2 / (1.0 - 0.95**STEP)) + 1e-08) + 0.1 * master
    return master - 0.01 * update, new_m1, new_m2


def reduce_step_gather(weights, x_rows, dy_rows, master, m1, m2):
    f32, bf16 = jnp.float32, jnp.bfloat16
    vmem = pl.BlockSpec(memory_space=pltpu.VMEM)
    dma = pltpu.SemaphoreType.DMA
    tokens = x_rows.shape[0]
    blocks = pltpu.VMEM((NZ, NX, ROWS, WIDTH), bf16)
    wide = pltpu.VMEM((NZ, ROWS, WIDTH), bf16)
    half = pltpu.VMEM((NZ, ROWS // 2, WIDTH), bf16)
    ring = pltpu.VMEM((6, ROWS, WIDTH), f32)
    acts = pltpu.VMEM((tokens, WIDTH), f32)
    peers = (NC * NZ - 1) + (NX * NY - 1)
    return pl.pallas_call(
        step_kernel,
        out_shape=(
            jax.ShapeDtypeStruct((ROWS, WIDTH), f32),
            jax.ShapeDtypeStruct((NX * NZ * NC, ROWS, WIDTH), bf16),
        ),
        in_specs=[pl.BlockSpec(memory_space=pltpu.HBM)] * 6,
        out_specs=(vmem, vmem),
        scratch_shapes=[
            pltpu.VMEM(weights.shape, bf16),
            pltpu.VMEM((2, *x_rows.shape), bf16),
            acts, acts, acts,
            pltpu.VMEM((3, tokens, WIDTH), bf16),
            pltpu.VMEM((3, ROWS, WIDTH), f32),
            pltpu.VMEM((NZ, NX, ROWS, WIDTH), f32),
            blocks, blocks,
            wide, half, half, wide, wide, wide, wide,
            ring, ring, ring, ring,
            pltpu.VMEM((3, 1, 128), f32),
            pltpu.VMEM((peers, 1, 128), f32),
            dma((5 * CHUNKS,)), dma((3,)),
            dma((NZ,)), dma((NZ,)),
            dma((2, NZ)), dma((2, NZ)),
            dma((2, NZ)), dma((2, NZ)),
            dma((2, 6, 2)), dma((2, 6, 2)),
            dma((peers,)), dma((peers,)),
            dma((2, 6)), dma((2, 6)),
            dma((4, NZ)), dma((4, NZ)),
            dma((NZ, 4)), dma((NZ, 4)),
        ],
        compiler_params=pltpu.CompilerParams(
            collective_id=0, has_side_effects=True, vmem_limit_bytes=34 << 20
        ),
    )(*(pltpu.with_memory_space_constraint(v, pltpu.HBM) for v in (weights, x_rows, dy_rows, master, m1, m2)))


def local(weights, inputs, out_grads, master, moment1, moment2):
    clipped, gathered = reduce_step_gather(
        weights[0], inputs[0], out_grads[0], master[0], moment1[0], moment2[0]
    )
    outs = adam(clipped[None], master, moment1, moment2)
    return (*outs, gathered.reshape(weights.shape))


def solution(mesh):
    split = Mesh(
        mesh.devices.reshape(NX, NZ, NC, mesh.shape["section"]), ("dp_0", "dp_1", "dp_2", "section")
    )
    shard = P("section", DP, None)
    whole = P("section", None, None)
    return jax.shard_map(
        local,
        mesh=split,
        in_specs=(whole, shard, shard, shard, shard, shard),
        out_specs=(shard, shard, shard, whole),
        check_vma=False,
    )
```
